32 devices in a mesh: slab: 4 (over x, core), panel: 8 (over z, y).
Axes of the slice: x: 2, y: 2, z: 4, core: 2. Of those that a mesh axis runs over, the one named last changes fastest.
Arguments:
- ranges: float32 [4, 4, 1024, 1024], P('slab', None, 'panel'), may hold values from -1.5 to 1.5
- pattern: int32 [4, 4, 16, 16], P('slab'), may hold values 0 or 1
Outputs:
- combined: float32 [4, 4, 1024, 1024], P('slab', None, 'panel')
The draws below stay inside these ranges and needn't reach their ends.
All inputs are finite; a program needn't handle non-finite values. No bound on the sum of `pattern` on one device may be relied on, other than what follows from the above.
Results may differ from the reference program's by a relative error of at most 0.01.
Values may be sent and summed in bfloat16 or wider, within the bound.
A program may use at most 64 MiB of HBM per device.

```python
import math
import jax
import jax.numpy as jnp
from jax import lax

M = 1024
BLK = 64
NS_ITERS = 2
LEVELS = 2
GROUPS = 4
NB = 16


def draw_ranges(key, part):
    noise_key = jax.random.fold_in(key, 0)
    sign_key = jax.random.fold_in(key, 1)
    size_key = jax.random.fold_in(key, 2)
    turn_key = jax.random.fold_in(key, 4)
    spread_vals = jnp.clip(jax.random.normal(noise_key, (GROUPS, 4, M, M), jnp.float32), -6.0, 6.0)
    off_part = spread_vals * (0.25 / math.sqrt(M))
    reflect_sign = jnp.where(jax.random.bernoulli(sign_key, 0.5, (GROUPS, M)), 1.0, -1.0)
    carry_sign = jnp.where(jax.random.bernoulli(turn_key, 0.5, (GROUPS, M)), 1.0, -1.0)
    reflect = jax.random.uniform(size_key, (GROUPS, M), jnp.float32, 0.4, 0.7)
    carry = jnp.sqrt(1.0 - reflect * reflect)
    diag_vals = jnp.stack([reflect_sign * reflect, carry_sign * carry, carry_sign * carry, -reflect_sign * reflect], axis=1)
    diagonal = jnp.eye(M, dtype=jnp.float32)[None, None, :, :] * diag_vals[:, :, :, None]
    return (off_part + diagonal).astype(jnp.float32)


def set_ends(values, own_key, least, top_value):
    extent = values.shape
    spot = [jax.random.randint(jax.random.fold_in(own_key, axis), (), 0, extent[axis]) for axis in range(len(extent))]
    values = values.at[tuple(spot)].set(least)
    longest = extent.index(max(extent))
    spot[longest] = (spot[longest] + 1) % extent[longest]
    return values.at[tuple(spot)].set(top_value)


def setup_inputs(seed: int = 0) -> dict:
    arg_keys = jax.random.split(jax.random.key(seed), 3)
    return {
        "ranges": draw_ranges(jax.random.fold_in(arg_keys[2], 71), 0),
        "pattern": set_ends((jax.random.randint(arg_keys[1], (GROUPS, 4, NB, NB), 0, 4) < 3).astype(jnp.int32), jax.random.fold_in(arg_keys[1], 1), 0, 1),
    }


def to_half(values):
    return values.astype(jnp.bfloat16)


def multiply(left, right):
    return jnp.dot(to_half(left), to_half(right), preferred_element_type=jnp.float32)


def star(head, tail):
    head_top, head_up, head_down, head_bottom = head[0], head[1], head[2], head[3]
    tail_top, tail_up, tail_down, tail_bottom = tail[0], tail[1], tail[2], tail[3]
    identity = jnp.eye(M, dtype=jnp.float32)
    loop_term = multiply(tail_top, head_bottom)
    loop_kept = lax.optimization_barrier(to_half(loop_term)).astype(jnp.float32)
    defect = identity - loop_kept
    guess = identity + loop_kept
    for newton_step in range(2, NS_ITERS + 1):
        guess = 2.0 * guess - multiply(multiply(guess, defect), guess)
    lifted = multiply(head_up, guess)
    joint_up = multiply(lifted, tail_up)
    bounce = multiply(tail_top, head_down)
    joint_top = head_top + multiply(lifted, bounce)
    reach = multiply(tail_down, head_bottom)
    through = multiply(reach, guess)
    joint_down = multiply(tail_down, head_down) + multiply(through, bounce)
    joint_bottom = tail_bottom + multiply(reach, tail_up) + multiply(multiply(through, loop_term), tail_up)
    return jnp.stack([joint_top, joint_up, joint_down, joint_bottom])


def reference(ranges, pattern):
    block_mask = jnp.repeat(jnp.repeat(pattern.astype(jnp.float32), BLK, axis=2), BLK, axis=3)
    merged = [ranges[group_id] * block_mask[group_id] for group_id in range(GROUPS)]
    for tree_level in range(LEVELS):
        span_size = 2 ** tree_level
        outcome = list(merged)
        for low_group in range(GROUPS):
            if (low_group // span_size) % 2 == 0:
                result = star(merged[low_group], merged[low_group + span_size])
                outcome[low_group] = result
                outcome[low_group + span_size] = result
        merged = outcome
    return jnp.stack(merged)
```

```python
import functools
import jax
import jax.numpy as jnp
from jax import lax
from jax.experimental import pallas as pl
from jax.experimental.pallas import tpu as pltpu
from jax.sharding import PartitionSpec as P

BLK = 64
MESH = pl.DeviceIdType.MESH


def merged(*streams):
    events = []
    for order, (items, start, end) in enumerate(streams):
        for i, item in enumerate(items):
            events.append((start + (end - start) * (i + 0.5) / len(items), order, i, item))
    return [event[-1] for event in sorted(events, key=lambda event: event[:3])]


def kernel(outer, inner, counts, first_ref, second_ref, left_ref, add_ref, out_ref,
           right, swap, hold, base, front, mid, recv_sem, send_sem, swap_sem, local_sem, last_recv, last_send):
    rows, width = left_ref.shape
    panels = outer * inner
    reach = panels // 2
    piece = rows // 2
    wing = width // 2
    slab = lax.axis_index("slab")
    panel = lax.axis_index("panel")
    core = slab % 2
    side = (slab // 2) % 2
    chip = slab - core
    far_chip = chip + 2 - 4 * side
    sibling = (chip + 1 - core, panel)
    partner = (far_chip + core, panel)
    gives = (side + core) % 2
    turn_way = 1 - 2 * core
    is_tail = core == 1
    is_giver = gives == 1
    is_taker = gives == 0

    column = panel % inner
    rise = panel // inner
    spot_here = column * outer + rise + (outer - 1 - 2 * rise) * (column % 2)

    def at_ring(shift):
        where = (spot_here + shift + panels) % panels
        turn = where // outer
        step = where % outer
        return (step + (outer - 1 - 2 * step) * (turn % 2)) * inner + turn

    beside = {1: at_ring(1), -1: at_ring(-1)}

    barrier = pltpu.get_barrier_semaphore()
    friends = [(chip + half, beside[way]) for way in (1, -1) for half in range(2)]
    friends += [(far_chip + half, panel) for half in range(2)] + [sibling]
    for friend in friends:
        pl.semaphore_signal(barrier, inc=1, device_id=friend, device_id_type=MESH)
    pl.semaphore_wait(barrier, len(friends))

    sent = []
    LATE, REST = 3, 7
    wings = {LATE: 0, REST: wing}

    def block(m, row, count):
        span = pl.ds(pl.multiple_of(row, count), count)
        if isinstance(m, int) and m in wings:
            return right.at[LATE, span, pl.ds(wings[m], wing)]
        return right.at[m, span, :]

    def place(m, p, half):
        return block(m, p * rows + half * piece, piece)

    def own_rows(m):
        return block(m, panel * rows, rows)

    def push(m, src, p, half, target, guard=None):
        spot = len(sent)
        sent.append((guard, m))
        pltpu.make_async_remote_copy(
            src_ref=src, dst_ref=place(m, p, half), send_sem=send_sem.at[spot],
            recv_sem=recv_sem.at[m, p, half], device_id=target, device_id_type=MESH).start()

    def arrive(m, p, half):
        spot = place(m, p, half)
        pltpu.make_async_remote_copy(
            src_ref=spot, dst_ref=spot, send_sem=send_sem.at[0], recv_sem=recv_sem.at[m, p, half],
            device_id=sibling, device_id_type=MESH).wait_recv()

    def local_copy(m, src):
        return pltpu.make_async_copy(src, own_rows(m), local_sem.at[m])

    def open_ring(m, src, guard=None, across=False):
        parts = [src.at[pl.ds(half * piece, piece), :] for half in range(2)]
        for half in range(2):
            for way in (1, -1):
                push(m, parts[half], panel, half, (chip + half, beside[way]), guard)
            if across:
                push(m, parts[half], panel, half, (far_chip + half, panel), guard)
        for half in range(2):
            push(m, parts[half], panel, half, sibling, guard)

    def spread(distance):
        return [turn_way, -turn_way] if distance < reach else [turn_way]

    def relay(m, distance, across=False):
        for i, way in enumerate(spread(distance)):
            p = at_ring(-way * distance)
            arrive(m, p, core)
            src = place(m, p, core)
            if distance + 1 < reach or (distance + 1 == reach and i == 0):
                push(m, src, p, core, (slab, at_ring(way)))
            if across:
                push(m, src, p, core, partner)
            push(m, src, p, core, sibling)

    def relay_far(m, distance):
        for way in spread(distance) if distance else [1]:
            p = at_ring(-way * distance)
            arrive(m, p, core)
            push(m, place(m, p, core), p, core, sibling)

    def settle(m, far=False):
        if far:
            arrive(m, panel, 1 - core)
        for distance in range(1, reach + 1):
            for way in (1, -1) if distance < reach else (1,):
                arrive(m, at_ring(-way * distance), 1 - core)

    def settle_own(m, absent):
        @pl.when(absent)
        def _():
            for half in range(2):
                arrive(m, panel, half)

    def product(left, factor, emit, cols=None):
        cols = slice(None) if cols is None else cols
        emit(cols, jnp.dot(left[...], factor[:, cols], preferred_element_type=jnp.float32))

    def keep(ref):
        def emit(cols, value):
            ref[:, cols] = value.astype(ref.dtype)
        return emit

    def keep_sum(ref, extra):
        def emit(cols, value):
            ref[:, cols] = (extra[:, cols].astype(jnp.float32) + value).astype(ref.dtype)
        return emit

    def swap_copy():
        return pltpu.make_async_remote_copy(
            src_ref=swap, dst_ref=swap, send_sem=swap_sem.at[0],
            recv_sem=swap_sem.at[1], device_id=partner, device_id_type=MESH)

    def chain(left, top, bottom, work, kept):
        count = len(work)

        def some(turn):
            while work and len(work) > count - (turn + 1) * count // 4:
                work.pop(0)()

        @pl.when(is_tail)
        def _():
            product(left, bottom, keep(base))

        @pl.when(core == 0)
        def _():
            base[...] = left[...]

        for turn in range(3):
            product(base if turn == 0 else front, top, keep(mid))
            some(turn)
            product(mid, bottom, keep_sum(front, base))
        product(front, top, keep(mid))
        some(3)

        @pl.when(is_tail)
        def _():
            front[...] = (left[...].astype(jnp.float32) + mid[...].astype(jnp.float32)).astype(front.dtype)
            product(mid, bottom, keep_sum(kept, base))

        @pl.when(core == 0)
        def _():
            kept[...] = mid[...]

    def later(action, *args):
        return lambda: action(*args)

    def relays(m, start, end):
        return [later(relay, m, distance) for distance in range(start, end)]

    def run(actions):
        for action in actions:
            action()

    def open_early():
        @pl.when(is_giver)
        def _():
            open_ring(2, second_ref, "gives")
            local_copy(2, second_ref).start()

    def open_late(m):
        @pl.when(is_taker)
        def _():
            part = second_ref.at[:, pl.ds(wings[m], wing)]
            open_ring(m, part, "takes")
            local_copy(m, part).start()

    quarter = max(reach // 4, 1)
    open_ring(core, first_ref)
    local_copy(core, first_ref).start()
    run(merged(
        ([later(relay, m, distance) for distance in range(1, reach + 1) for m in range(2)], 0, 1),
        ([open_early], 0.4, 0.5), (relays(2, 1, quarter + 1), 0.7, 0.8), ([later(open_late, LATE)], 0.75, 0.8)))
    for m in range(2):
        settle(m)
    local_copy(core, first_ref).wait()
    for half in range(2):
        arrive(1 - core, panel, half)
    chain(left_ref, right.at[1], right.at[0], merged(
        (relays(2, quarter + 1, 3 * quarter + 1), 0, 1), (relays(LATE, 1, quarter + 1), 0.3, 0.7)), hold)
    mine, far, extra = 4 + side, 5 - side, 6

    @pl.when(is_giver)
    def _():
        own_rows(extra)[...] = front[...]
        open_ring(extra, own_rows(extra), "gives")

    run(merged(
        (relays(2, 3 * quarter + 1, reach + 1), 0, 1), (relays(LATE, quarter + 1, 2 * quarter + 1), 0, 0.5)))
    settle(2)
    settle_own(2, is_taker)

    @pl.when(is_giver)
    def _():
        local_copy(2, second_ref).wait()
        product(hold, right.at[2], keep_sum(own_rows(mine), add_ref))
        open_ring(mine, own_rows(mine), "gives", True)

    @pl.when(is_taker)
    def _():
        product(front, right.at[2], keep(swap))
        swap_copy().start()

    kind = [later(relay, mine, 1, True), later(relay_far, far, 0)]
    for distance in range(2, reach + 1):
        kind += [later(relay, mine, distance, True), later(relay_far, far, distance - 1)]
    kind += [later(relay_far, far, reach)]
    run(merged(
        (kind, 0, 1), (relays(extra, 1, 3 * quarter + 1), 0, 0.8), (relays(LATE, 2 * quarter + 1, reach + 1), 0, 0.5),
        ([later(open_late, REST)] + relays(REST, 1, 2 * quarter + 1), 0.2, 1)))
    settle(mine)
    settle(far, True)
    settle_own(mine, is_taker)

    @pl.when(is_giver)
    def _():
        swap_copy().wait_recv()

    chain(swap, right.at[5], right.at[4], merged((relays(extra, 3 * quarter + 1, reach + 1), 0, 1), (relays(REST, 2 * quarter + 1, 3 * quarter + 1), 0, 1)), base)
    run([])
    settle(extra)
    settle_own(extra, is_taker)

    @pl.when(is_giver)
    def _():
        product(front, right.at[extra], keep(mid))

    @pl.when(is_taker)
    def _():
        product(base, right.at[extra], keep_sum(mid, hold))

    here = 2 * core + side
    across = 2 * core + 1 - side

    def last_copy(m, kind):
        cols = pl.ds(wings[m], wing)
        spot = 3 * (m == REST) + kind
        ref = out_ref.at[across if kind == 2 else here, :, cols]
        return pltpu.make_async_remote_copy(
            src_ref=ref, dst_ref=ref, send_sem=last_send.at[spot], recv_sem=last_recv.at[spot],
            device_id=partner if kind == 0 else sibling, device_id_type=MESH)

    for m in (LATE, REST):
        if m == REST:
            run(relays(REST, 3 * quarter + 1, reach + 1))
        settle(m)
        settle_own(m, is_giver)
        cols = slice(wings[m], wings[m] + wing)

        @pl.when(is_giver)
        def _():
            product(mid, right.at[LATE], keep(out_ref.at[here]), cols)

        @pl.when(is_taker)
        def _():
            local_copy(m, second_ref.at[:, pl.ds(wings[m], wing)]).wait()
            product(mid, right.at[LATE], keep_sum(out_ref.at[here], add_ref), cols)

        last_copy(m, 0).start()
        last_copy(m, 1).start()
    for m in (LATE, REST):
        last_copy(m, 0).wait_recv()
        last_copy(m, 2).start()

    @pl.when(is_taker)
    def _():
        swap_copy().wait_send()

    def drain(guard):
        for spot, (kept, m) in enumerate(sent):
            if kept == guard:
                own = place(m if isinstance(m, int) else 0, 0, 0)
                pltpu.make_async_remote_copy(
                    src_ref=own, dst_ref=own, send_sem=send_sem.at[spot], recv_sem=recv_sem.at[0, 0, 0],
                    device_id=sibling, device_id_type=MESH).wait_send()

    drain(None)
    pl.when(is_giver)(lambda: drain("gives"))
    pl.when(is_taker)(lambda: drain("takes"))
    for m in (LATE, REST):
        last_copy(m, 0).wait_send()
        last_copy(m, 1).wait()
        last_copy(m, 2).wait()
    assert len(sent) <= counts, len(sent)


def body(panels, ranges, pattern):
    blocks = ranges[0]
    rows, width = blocks.shape[1:]
    count = pattern.shape[2]
    core = lax.axis_index("slab") % 2
    row_start = lax.axis_index("panel") * rows
    row_ids = row_start + jnp.arange(rows, dtype=jnp.int32)
    col_ids = jnp.arange(width, dtype=jnp.int32)
    block_ids = jnp.arange(count, dtype=jnp.int32)
    row_pick = (row_ids[:, None] // BLK == block_ids[None, :]).astype(jnp.float32)
    col_pick = (block_ids[:, None] == col_ids[None, :] // BLK).astype(jnp.float32)
    mask = jnp.einsum("mi,gij,jc->gmc", row_pick, pattern[0].astype(jnp.float32), col_pick)
    masked = blocks * mask
    half = masked.astype(jnp.bfloat16)
    head = core == 0
    first = jnp.where(head, half[3], half[0])
    second = jnp.where(head, half[2], half[1])
    left = jnp.where(head, half[1], half[2])
    add = jnp.where(head, masked[0], masked[3])

    outer = min(4, panels)
    inner = panels // outer
    counts = 24 * panels
    vmem = pl.BlockSpec(memory_space=pltpu.VMEM)
    out = pl.pallas_call(
        functools.partial(kernel, outer, inner, counts),
        out_shape=jax.ShapeDtypeStruct((4, rows, width), jnp.bfloat16),
        in_specs=[vmem] * 4,
        out_specs=vmem,
        scratch_shapes=[
            pltpu.VMEM((7, width, width), jnp.bfloat16),
            *[pltpu.VMEM((rows, width), jnp.bfloat16)] * 5,
            pltpu.SemaphoreType.DMA((8, panels, 2)),
            pltpu.SemaphoreType.DMA((counts,)),
            pltpu.SemaphoreType.DMA((2,)),
            pltpu.SemaphoreType.DMA((8,)),
            pltpu.SemaphoreType.DMA((6,)),
            pltpu.SemaphoreType.DMA((6,)),
        ],
        compiler_params=pltpu.CompilerParams(
            collective_id=0, has_side_effects=True, vmem_limit_bytes=48 << 20),
        name="merge_levels",
    )(first, second, left, add)
    return out.astype(jnp.float32)[None]


def solution(mesh):
    return jax.shard_map(
        functools.partial(body, mesh.shape["panel"]),
        mesh=mesh,
        in_specs=(P("slab", None, "panel", None), P("slab", None, None, None)),
        out_specs=P("slab", None, "panel", None),
        check_vma=False,
    )
```

```python
import functools
import jax
import jax.numpy as jnp
from jax import lax
from jax.experimental import pallas as pl
from jax.experimental.pallas import tpu as pltpu
from jax.sharding import PartitionSpec as P

BLK = 64
MESH = pl.DeviceIdType.MESH


def merged(*streams):
    events = []
    for order, (items, start, end) in enumerate(streams):
        for i, item in enumerate(items):
            events.append((start + (end - start) * (i + 0.5) / len(items), order, i, item))
    return [event[-1] for event in sorted(events, key=lambda event: event[:3])]


def kernel(outer, inner, counts, first_ref, second_ref, left_ref, add_ref, out_ref,
           right, swap, hold, base, front, mid, recv_sem, send_sem, swap_sem, local_sem, last_recv, last_send):
    rows, width = left_ref.shape
    panels = outer * inner
    reach = panels // 2
    piece = rows // 2
    wing = width // 2
    slab = lax.axis_index("slab")
    panel = lax.axis_index("panel")
    core = slab % 2
    side = (slab // 2) % 2
    chip = slab - core
    far_chip = chip + 2 - 4 * side
    sibling = (chip + 1 - core, panel)
    partner = (far_chip + core, panel)
    gives = (side + core) % 2
    turn_way = 1 - 2 * core
    is_tail = core == 1
    is_giver = gives == 1
    is_taker = gives == 0

    column = panel % inner
    rise = panel // inner
    spot_here = column * outer + rise + (outer - 1 - 2 * rise) * (column % 2)

    def at_ring(shift):
        where = (spot_here + shift + panels) % panels
        turn = where // outer
        step = where % outer
        return (step + (outer - 1 - 2 * step) * (turn % 2)) * inner + turn

    beside = {1: at_ring(1), -1: at_ring(-1)}

    barrier = pltpu.get_barrier_semaphore()
    friends = [(chip + half, beside[way]) for way in (1, -1) for half in range(2)]
    friends += [(far_chip + half, panel) for half in range(2)] + [sibling]
    for friend in friends:
        pl.semaphore_signal(barrier, inc=1, device_id=friend, device_id_type=MESH)
    pl.semaphore_wait(barrier, len(friends))

    sent = []
    LATE, REST = 3, 7
    wings = {LATE: 0, REST: wing}

    def block(m, row, count):
        span = pl.ds(pl.multiple_of(row, count), count)
        if isinstance(m, int) and m in wings:
            return right.at[LATE, span, pl.ds(wings[m], wing)]
        return right.at[m, span, :]

    def place(m, p, half):
        return block(m, p * rows + half * piece, piece)

    def own_rows(m):
        return block(m, panel * rows, rows)

    def push(m, src, p, half, target, guard=None):
        spot = len(sent)
        sent.append((guard, m))
        pltpu.make_async_remote_copy(
            src_ref=src, dst_ref=place(m, p, half), send_sem=send_sem.at[spot],
            recv_sem=recv_sem.at[m, p, half], device_id=target, device_id_type=MESH).start()

    def arrive(m, p, half):
        spot = place(m, p, half)
        pltpu.make_async_remote_copy(
            src_ref=spot, dst_ref=spot, send_sem=send_sem.at[0], recv_sem=recv_sem.at[m, p, half],
            device_id=sibling, device_id_type=MESH).wait_recv()

    def local_copy(m, src):
        return pltpu.make_async_copy(src, own_rows(m), local_sem.at[m])

    def open_ring(m, src, guard=None, across=False):
        parts = [src.at[pl.ds(half * piece, piece), :] for half in range(2)]
        for half in range(2):
            for way in (1, -1):
                push(m, parts[half], panel, half, (chip + half, beside[way]), guard)
            if across:
                push(m, parts[half], panel, half, (far_chip + half, panel), guard)
        for half in range(2):
            push(m, parts[half], panel, half, sibling, guard)

    def spread(distance):
        return [turn_way, -turn_way] if distance < reach else [turn_way]

    def relay(m, distance, across=False):
        for i, way in enumerate(spread(distance)):
            p = at_ring(-way * distance)
            arrive(m, p, core)
            src = place(m, p, core)
            if distance + 1 < reach or (distance + 1 == reach and i == 0):
                push(m, src, p, core, (slab, at_ring(way)))
            if across and not by_ring(distance):
                push(m, src, p, core, partner)
            push(m, src, p, core, sibling)

    def by_ring(distance):
        return distance == reach

    def relay_far(m, distance):
        for i, way in enumerate(spread(distance) if distance else [1]):
            p = at_ring(-way * distance)
            arrive(m, p, core)
            src = place(m, p, core)
            if by_ring(distance + 1):
                if distance == 0:
                    push(m, src, p, core, (slab, beside[1]))
                    push(m, src, p, core, (slab, beside[-1]))
                elif distance + 1 < reach or (distance + 1 == reach and i == 0):
                    push(m, src, p, core, (slab, at_ring(way)))
            push(m, src, p, core, sibling)

    def settle(m, far=False):
        if far:
            arrive(m, panel, 1 - core)
        for distance in range(1, reach + 1):
            for way in (1, -1) if distance < reach else (1,):
                arrive(m, at_ring(-way * distance), 1 - core)

    def settle_own(m, absent):
        @pl.when(absent)
        def _():
            for half in range(2):
                arrive(m, panel, half)

    def product(left, factor, emit, cols=None):
        cols = slice(None) if cols is None else cols
        emit(cols, jnp.dot(left[...], factor[:, cols], preferred_element_type=jnp.float32))

    def keep(ref):
        def emit(cols, value):
            ref[:, cols] = value.astype(ref.dtype)
        return emit

    def keep_sum(ref, extra):
        def emit(cols, value):
            ref[:, cols] = (extra[:, cols].astype(jnp.float32) + value).astype(ref.dtype)
        return emit

    def swap_copy():
        return pltpu.make_async_remote_copy(
            src_ref=swap, dst_ref=swap, send_sem=swap_sem.at[0],
            recv_sem=swap_sem.at[1], device_id=partner, device_id_type=MESH)

    def chain(left, top, bottom, work, kept):
        count = len(work)

        def some(turn):
            while work and len(work) > count - (turn + 1) * count // 4:
                work.pop(0)()

        @pl.when(is_tail)
        def _():
            product(left, bottom, keep(base))

        @pl.when(core == 0)
        def _():
            base[...] = left[...]

        for turn in range(3):
            product(base if turn == 0 else front, top, keep(mid))
            some(turn)
            product(mid, bottom, keep_sum(front, base))
        product(front, top, keep(mid))
        some(3)

        @pl.when(is_tail)
        def _():
            front[...] = (left[...].astype(jnp.float32) + mid[...].astype(jnp.float32)).astype(front.dtype)
            product(mid, bottom, keep_sum(kept, base))

        @pl.when(core == 0)
        def _():
            kept[...] = mid[...]

    def later(action, *args):
        return lambda: action(*args)

    def relays(m, start, end):
        return [later(relay, m, distance) for distance in range(start, end)]

    def run(actions):
        for action in actions:
            action()

    def open_early():
        @pl.when(is_giver)
        def _():
            open_ring(2, second_ref, "gives")
            local_copy(2, second_ref).start()

    def open_late(m):
        @pl.when(is_taker)
        def _():
            part = second_ref.at[:, pl.ds(wings[m], wing)]
            open_ring(m, part, "takes")
            local_copy(m, part).start()

    quarter = max(reach // 4, 1)
    open_ring(core, first_ref)
    local_copy(core, first_ref).start()
    run(merged(
        ([later(relay, m, distance) for distance in range(1, reach + 1) for m in range(2)], 0, 1),
        ([open_early], 0.4, 0.5), (relays(2, 1, quarter + 1), 0.7, 0.8), ([later(open_late, LATE)], 0.75, 0.8)))
    for m in range(2):
        settle(m)
    local_copy(core, first_ref).wait()
    for half in range(2):
        arrive(1 - core, panel, half)
    chain(left_ref, right.at[1], right.at[0], merged(
        (relays(2, quarter + 1, 3 * quarter + 1), 0, 1), (relays(LATE, 1, quarter + 1), 0.3, 0.7)), hold)
    mine, far, extra = 4 + side, 5 - side, 6

    @pl.when(is_giver)
    def _():
        own_rows(extra)[...] = front[...]
        open_ring(extra, own_rows(extra), "gives")

    run(merged(
        (relays(2, 3 * quarter + 1, reach + 1), 0, 1), (relays(LATE, quarter + 1, 2 * quarter + 1), 0, 0.5)))
    settle(2)
    settle_own(2, is_taker)

    @pl.when(is_giver)
    def _():
        local_copy(2, second_ref).wait()
        product(hold, right.at[2], keep_sum(own_rows(mine), add_ref))
        open_ring(mine, own_rows(mine), "gives", True)

    @pl.when(is_taker)
    def _():
        product(front, right.at[2], keep(swap))
        swap_copy().start()

    kind = [later(relay, mine, 1, True), later(relay_far, far, 0)]
    for distance in range(2, reach + 1):
        kind += [later(relay, mine, distance, True), later(relay_far, far, distance - 1)]
    kind += [later(relay_far, far, reach)]
    run(merged(
        (kind, 0, 1), (relays(extra, 1, 3 * quarter + 1), 0, 0.8), (relays(LATE, 2 * quarter + 1, reach + 1), 0, 0.5),
        ([later(open_late, REST)] + relays(REST, 1, 2 * quarter + 1), 0.2, 1)))
    settle(mine)
    settle(far, True)
    settle_own(mine, is_taker)

    @pl.when(is_giver)
    def _():
        swap_copy().wait_recv()

    chain(swap, right.at[5], right.at[4], merged((relays(extra, 3 * quarter + 1, reach + 1), 0, 1), (relays(REST, 2 * quarter + 1, 3 * quarter + 1), 0, 1)), base)
    run([])
    settle(extra)
    settle_own(extra, is_taker)

    @pl.when(is_giver)
    def _():
        product(front, right.at[extra], keep(mid))

    @pl.when(is_taker)
    def _():
        product(base, right.at[extra], keep_sum(mid, hold))

    here = 2 * core + side
    across = 2 * core + 1 - side

    def last_copy(m, kind):
        cols = pl.ds(wings[m], wing)
        spot = 3 * (m == REST) + kind
        ref = out_ref.at[across if kind == 2 else here, :, cols]
        return pltpu.make_async_remote_copy(
            src_ref=ref, dst_ref=ref, send_sem=last_send.at[spot], recv_sem=last_recv.at[spot],
            device_id=partner if kind == 0 else sibling, device_id_type=MESH)

    for m in (LATE, REST):
        if m == REST:
            run(relays(REST, 3 * quarter + 1, reach + 1))
        settle(m)
        settle_own(m, is_giver)
        cols = slice(wings[m], wings[m] + wing)

        @pl.when(is_giver)
        def _():
            product(mid, right.at[LATE], keep(out_ref.at[here]), cols)

        @pl.when(is_taker)
        def _():
            local_copy(m, second_ref.at[:, pl.ds(wings[m], wing)]).wait()
            product(mid, right.at[LATE], keep_sum(out_ref.at[here], add_ref), cols)

        last_copy(m, 0).start()
        last_copy(m, 1).start()
    for m in (LATE, REST):
        last_copy(m, 0).wait_recv()
        last_copy(m, 2).start()

    @pl.when(is_taker)
    def _():
        swap_copy().wait_send()

    def drain(guard):
        for spot, (kept, m) in enumerate(sent):
            if kept == guard:
                own = place(m if isinstance(m, int) else 0, 0, 0)
                pltpu.make_async_remote_copy(
                    src_ref=own, dst_ref=own, send_sem=send_sem.at[spot], recv_sem=recv_sem.at[0, 0, 0],
                    device_id=sibling, device_id_type=MESH).wait_send()

    drain(None)
    pl.when(is_giver)(lambda: drain("gives"))
    pl.when(is_taker)(lambda: drain("takes"))
    for m in (LATE, REST):
        last_copy(m, 0).wait_send()
        last_copy(m, 1).wait()
        last_copy(m, 2).wait()
    assert len(sent) <= counts, len(sent)


def body(panels, ranges, pattern):
    blocks = ranges[0]
    rows, width = blocks.shape[1:]
    count = pattern.shape[2]
    core = lax.axis_index("slab") % 2
    row_start = lax.axis_index("panel") * rows
    row_ids = row_start + jnp.arange(rows, dtype=jnp.int32)
    col_ids = jnp.arange(width, dtype=jnp.int32)
    block_ids = jnp.arange(count, dtype=jnp.int32)
    row_pick = (row_ids[:, None] // BLK == block_ids[None, :]).astype(jnp.float32)
    col_pick = (block_ids[:, None] == col_ids[None, :] // BLK).astype(jnp.float32)
    mask = jnp.einsum("mi,gij,jc->gmc", row_pick, pattern[0].astype(jnp.float32), col_pick)
    masked = blocks * mask
    half = masked.astype(jnp.bfloat16)
    head = core == 0
    first = jnp.where(head, half[3], half[0])
    second = jnp.where(head, half[2], half[1])
    left = jnp.where(head, half[1], half[2])
    add = jnp.where(head, masked[0], masked[3])

    outer = min(4, panels)
    inner = panels // outer
    counts = 24 * panels
    vmem = pl.BlockSpec(memory_space=pltpu.VMEM)
    out = pl.pallas_call(
        functools.partial(kernel, outer, inner, counts),
        out_shape=jax.ShapeDtypeStruct((4, rows, width), jnp.bfloat16),
        in_specs=[vmem] * 4,
        out_specs=vmem,
        scratch_shapes=[
            pltpu.VMEM((7, width, width), jnp.bfloat16),
            *[pltpu.VMEM((rows, width), jnp.bfloat16)] * 5,
            pltpu.SemaphoreType.DMA((8, panels, 2)),
            pltpu.SemaphoreType.DMA((counts,)),
            pltpu.SemaphoreType.DMA((2,)),
            pltpu.SemaphoreType.DMA((8,)),
            pltpu.SemaphoreType.DMA((6,)),
            pltpu.SemaphoreType.DMA((6,)),
        ],
        compiler_params=pltpu.CompilerParams(
            collective_id=0, has_side_effects=True, vmem_limit_bytes=48 << 20),
        name="merge_levels",
    )(first, second, left, add)
    return out.astype(jnp.float32)[None]


def solution(mesh):
    return jax.shard_map(
        functools.partial(body, mesh.shape["panel"]),
        mesh=mesh,
        in_specs=(P("slab", None, "panel", None), P("slab", None, None, None)),
        out_specs=P("slab", None, "panel", None),
        check_vma=False,
    )
```
